256 devices in a mesh: seq: 64 (over z, y, x_hi), tp: 4 (over x_lo, core).
Axes of the slice: x: 4 (x_hi: 2, x_lo: 2; x = x_hi * 2 + x_lo), y: 4, z: 8, core: 2. Of those that a mesh axis runs over, the one named last changes fastest.
Arguments:
- latents: bfloat16 [16384, 5120], P('seq', 'tp'), may hold values from -6 to 6
- noise: bfloat16 [16384, 5120], P('seq', 'tp'), may hold values from -6 to 6
- tstep: int32 [256], P('seq'), may hold values from 0 to 999
- offsets: int32 [256], P('seq'), may hold values from -64 to 64, as said below
- teacher_heads: bfloat16 [16384, 2560], P('seq', 'tp'), may hold values from -6 to 6
- teacher_proj: bfloat16 [2560, 5120], P('tp', 'seq'), may hold values from -0.125 to 0.125
- queries: bfloat16 [16384, 2560], P('seq', 'tp'), may hold values from -200 to 200
- keys: bfloat16 [16384, 2560], P('seq', 'tp'), may hold values from -6 to 6
- values: bfloat16 [16384, 2560], P('seq', 'tp'), may hold values from -6 to 6
- query_tangent: bfloat16 [16384, 2560], P('seq', 'tp'), may hold values from -6 to 6
- key_tangent: bfloat16 [16384, 2560], P('seq', 'tp'), may hold values from -6 to 6
- value_tangent: bfloat16 [16384, 2560], P('seq', 'tp'), may hold values from -6 to 6
- out_proj: bfloat16 [2560, 5120], P('tp', 'seq'), may hold values from -0.125 to 0.125
Outputs:
- student_out: float32 [16384, 5120], P('seq', 'tp')
- student_tangent: float32 [16384, 5120], P('seq', 'tp')
The draws below stay inside these ranges and needn't reach their ends.
Inputs may be any that keep to these rules, and one draw needn't show every extreme that they name: `offsets`: both ends, -64 and 64, occur in every draw.
All inputs are finite; a program needn't handle non-finite values.
Results may differ from the reference program's by a relative error of at most 0.0045.
Values may be sent and summed in bfloat16 or wider, within the bound.
No kernel may reach another device: no remote copies, remote signals or barrier semaphores. Data moves between devices by JAX's collectives and lax.ppermute only.
A program may use at most 128 MiB of HBM per device.

```python
import math
import jax
import jax.numpy as jnp
from jax import lax

D = 5120
HEADS = 20
HD = 128
WIN = 256
OFF = 64
BLK = 64
STEPS = 1000
TOKENS = 16384
HW = 2560
NB = 256


def query_key_pair(key):
    pair_key = jax.random.fold_in(key, 7301)
    key_first, key_second = jax.random.split(pair_key)
    query_draw = jax.random.normal(key_first, (TOKENS, HW), jnp.float32)
    keys_drawn = jnp.clip(jax.random.normal(key_second, (TOKENS, HW), jnp.float32), -5.5, 5.5)
    return (query_draw, keys_drawn)


def draw_queries(key, part):
    return query_key_pair(key)[0].astype(jnp.bfloat16)


def draw_keys(key, part):
    return query_key_pair(key)[1].astype(jnp.bfloat16)


def draw_offsets(key, part):
    base_key = jax.random.fold_in(key, 4409)
    key_base, key_first, key_gap = jax.random.split(base_key, 3)
    shifts = jax.random.randint(key_base, (NB,), -OFF, OFF + 1, dtype=jnp.int32)
    first_slot = jax.random.randint(key_first, (), 0, NB, dtype=jnp.int32)
    gap_slot = jax.random.randint(key_gap, (), 1, NB, dtype=jnp.int32)
    second_slot = (first_slot + gap_slot) % NB
    return shifts.at[first_slot].set(-OFF).at[second_slot].set(OFF)


def plant(entries, stream_key, low, largest):
    extent = entries.shape
    spot = [jax.random.randint(jax.random.fold_in(stream_key, axis), (), 0, extent[axis]) for axis in range(len(extent))]
    entries = entries.at[tuple(spot)].set(low)
    longest = extent.index(max(extent))
    spot[longest] = (spot[longest] + 1) % extent[longest]
    return entries.at[tuple(spot)].set(largest)


def block_levels(key, extent, pieces, low, top_value):
    factor_of, own = 1.0, jax.random.fold_in(key, 6)
    for dim, blocks in pieces:
        heights = jnp.exp(jax.random.uniform(jax.random.fold_in(own, dim), (blocks,), jnp.float32, low / len(pieces), top_value / len(pieces)))
        factor_of = factor_of * jnp.repeat(heights, extent[dim] // blocks).reshape([-1 if axis == dim else 1 for axis in range(len(extent))])
    return factor_of


def centred(own_key, shape, scale, limit, cuts=(), held_as=jnp.bfloat16):
    values = scale * jax.random.normal(own_key, shape, jnp.float32)
    if cuts:
        values = values * block_levels(own_key, shape, cuts, -0.22, 0.18)
    return jnp.clip(values, -limit, limit).astype(held_as)


def setup_inputs(seed: int = 0) -> dict:
    splits = jax.random.split(jax.random.key(seed), 14)
    return {
        "latents": centred(splits[0], (TOKENS, D), 1.0, 6.0, ((0, 64), (1, 4))),
        "noise": centred(splits[1], (TOKENS, D), 1.0, 6.0, ((0, 64), (1, 4))),
        "tstep": plant(jax.random.randint(splits[2], (NB,), 0, STEPS), jax.random.fold_in(splits[2], 1), 0, STEPS - 1).astype(jnp.int32),
        "offsets": draw_offsets(jax.random.fold_in(splits[13], 71), 0),
        "teacher_heads": centred(splits[4], (TOKENS, HW), 1.0, 6.0, ((0, 64), (1, 4))),
        "teacher_proj": centred(splits[5], (HW, D), HW ** -0.5, 0.125, ((0, 4), (1, 64))),
        "queries": draw_queries(jax.random.fold_in(splits[13], 71), 0),
        "keys": draw_keys(jax.random.fold_in(splits[13], 71), 0),
        "values": centred(splits[8], (TOKENS, HW), 1.0, 6.0, ((0, 64), (1, 4))),
        "query_tangent": centred(splits[9], (TOKENS, HW), 1.0, 6.0, ((0, 64), (1, 4))),
        "key_tangent": centred(splits[10], (TOKENS, HW), 1.0, 6.0, ((0, 64), (1, 4))),
        "value_tangent": centred(splits[11], (TOKENS, HW), 1.0, 6.0, ((0, 64), (1, 4))),
        "out_proj": centred(splits[12], (HW, D), HW ** -0.5, 0.125, ((0, 4), (1, 64))),
    }


def reference(latents, noise, tstep, offsets, teacher_heads, teacher_proj, queries, keys, values, query_tangent, key_tangent, value_tangent, out_proj):
    reach = WIN // 2 + OFF
    score_scale = 1.0 / math.sqrt(HD)
    step_time = (tstep.astype(jnp.float32) + 0.5) * (math.pi / (2 * STEPS))
    per_token = jnp.repeat(step_time, BLK)[:, None]
    cosine = jnp.cos(per_token)
    sine_t = jnp.sin(per_token)
    noisy = cosine * latents.astype(jnp.float32) + sine_t * noise.astype(jnp.float32)
    velocity = jnp.dot(teacher_heads, teacher_proj, preferred_element_type=jnp.float32)

    def padded_heads(array):
        return jnp.pad(array.reshape(TOKENS, HEADS, HD), ((reach, reach), (0, 0), (0, 0)))
    query_heads = queries.reshape(TOKENS, HEADS, HD)
    query_dots = query_tangent.reshape(TOKENS, HEADS, HD)
    key_pad = padded_heads(keys)
    value_pad = padded_heads(values)
    key_dot_pad = padded_heads(key_tangent)
    value_dot_pad = padded_heads(value_tangent)

    def one_block(block_index):
        row_start = block_index * BLK
        query_block = lax.dynamic_slice_in_dim(query_heads, row_start, BLK, 0).astype(jnp.float32)
        query_dot = lax.dynamic_slice_in_dim(query_dots, row_start, BLK, 0).astype(jnp.float32)
        span = BLK + 2 * reach
        key_block = lax.dynamic_slice_in_dim(key_pad, row_start, span, 0).astype(jnp.float32)
        value_block = lax.dynamic_slice_in_dim(value_pad, row_start, span, 0).astype(jnp.float32)
        key_dot = lax.dynamic_slice_in_dim(key_dot_pad, row_start, span, 0).astype(jnp.float32)
        value_dot = lax.dynamic_slice_in_dim(value_dot_pad, row_start, span, 0).astype(jnp.float32)
        query_pos = row_start + jnp.arange(BLK, dtype=jnp.int32)
        key_pos = row_start - reach + jnp.arange(span, dtype=jnp.int32)
        relative = key_pos[None, :] - query_pos[:, None]
        window_low = offsets[block_index] - WIN // 2
        inside = (relative >= window_low) & (relative < window_low + WIN)
        inside = inside & ((key_pos >= 0) & (key_pos < TOKENS))[None, :]
        scores = jnp.einsum('qhd,khd->hqk', query_block, key_block) * score_scale
        scores = jnp.where(inside[None], scores, -1e+30)
        peak_val = lax.optimization_barrier(jnp.max(scores, axis=-1, keepdims=True))
        expo_val = jnp.where(inside[None], jnp.exp(scores - peak_val), 0.0)
        weights = expo_val / lax.optimization_barrier(jnp.sum(expo_val, axis=-1, keepdims=True))
        score_dot = (jnp.einsum('qhd,khd->hqk', query_dot, key_block) + jnp.einsum('qhd,khd->hqk', query_block, key_dot)) * score_scale
        weight_dot = weights * (score_dot - lax.optimization_barrier(jnp.sum(weights * score_dot, axis=-1, keepdims=True)))
        weights_low = lax.optimization_barrier(weights.astype(jnp.bfloat16)).astype(jnp.float32)
        weight_dot_low = lax.optimization_barrier(weight_dot.astype(jnp.bfloat16)).astype(jnp.float32)
        attended = jnp.einsum('hqk,khd->qhd', weights_low, value_block)
        attended_dot = jnp.einsum('hqk,khd->qhd', weight_dot_low, value_block) + jnp.einsum('hqk,khd->qhd', weights_low, value_dot)
        return (attended.astype(jnp.bfloat16).reshape(BLK, HW), attended_dot.astype(jnp.bfloat16).reshape(BLK, HW))
    attended, attended_tangent = lax.map(one_block, jnp.arange(NB, dtype=jnp.int32))
    attended = attended.reshape(TOKENS, HW)
    attended_tangent = attended_tangent.reshape(TOKENS, HW)
    branch = jnp.dot(attended, out_proj, preferred_element_type=jnp.float32)
    branch_tangent = jnp.dot(attended_tangent, out_proj, preferred_element_type=jnp.float32)
    student_out = cosine * noisy - sine_t * branch
    student_tangent = -sine_t * noisy + cosine * velocity - cosine * branch - sine_t * branch_tangent
    return (student_out, student_tangent)
```

```python
import math

import jax
import jax.numpy as jnp
from jax import lax
from jax.experimental import pallas as pl
from jax.experimental.pallas import tpu as pltpu
from jax.sharding import PartitionSpec as P

HD = 128
WIN = 256
OFF = 64
BLK = 64
STEPS = 1000
REACH = WIN // 2 + OFF
AXES = ("seq", "tp")
NZ, NY, NX, NT = 8, 4, 2, 4
SPAN = 384


def flat(z, y, x, t):
    return (((z % NZ) * NY + y % NY) * NX + x % NX) * NT + t


def pairs(move):
    return [
        (flat(z, y, x, t), flat(*move(z, y, x, t)))
        for z in range(NZ)
        for y in range(NY)
        for x in range(NX)
        for t in range(NT)
    ]


def send(a, move):
    return lax.ppermute(a, AXES, pairs(move))


def z_by(d):
    return lambda z, y, x, t: (z + d, y, x, t)


def y_by(d):
    return lambda z, y, x, t: (z, y + d, x, t)


def t_xor(k):
    return lambda z, y, x, t: (z, y, x, t ^ k)


def swap_zt(flip):
    return lambda z, y, x, t: (t * 2 + (z & 1), y, x ^ flip, z >> 1)


def attn_kernel(where, offs, q, qd, k, v, kd, vd, low, high, out, pad, sems):
    tokens = q.shape[0]
    heads = q.shape[1] // HD
    copies = []
    for i, own in enumerate((k, v, kd, vd)):
        copies.append(pltpu.make_async_copy(own, pad.at[i, pl.ds(REACH, tokens)], sems.at[i]))
    copies.append(pltpu.make_async_copy(low, pad.at[:, pl.ds(0, REACH)], sems.at[4]))
    copies.append(pltpu.make_async_copy(high, pad.at[:, pl.ds(REACH + tokens, REACH)], sems.at[5]))
    for c in copies:
        c.start()
    for c in copies:
        c.wait()
    scale = 1.0 / math.sqrt(HD)
    first = where[0] * tokens
    total = where[1] * tokens
    nt = (((1,), (1,)), ((), ()))
    nn = (((1,), (0,)), ((), ()))

    def one_block(b, carry):
        off = offs[b]
        want = b * BLK + REACH + off - WIN // 2
        start = jnp.minimum((want // 16) * 16, tokens + 2 * REACH - SPAN)
        start = pl.multiple_of(start, 16)
        rows = pl.ds(pl.multiple_of(b * BLK, BLK), BLK)
        keys = pl.ds(start, SPAN)
        ki = lax.broadcasted_iota(jnp.int32, (BLK, SPAN), 1) + (start - REACH)
        qi = lax.broadcasted_iota(jnp.int32, (BLK, SPAN), 0) + b * BLK
        rel = ki - qi
        inside = (rel >= off - WIN // 2) & (rel < off + WIN // 2)
        inside = inside & (ki >= -first) & (ki < total - first)
        for h in range(heads):
            cols = slice(h * HD, (h + 1) * HD)
            qb = q[rows, cols]
            both = jnp.concatenate([qb, qd[rows, cols]], axis=0)
            kb = pad[0, keys, cols]
            s2 = lax.dot_general(both, kb, nt, preferred_element_type=jnp.float32)
            s3 = lax.dot_general(qb, pad[2, keys, cols], nt, preferred_element_type=jnp.float32)
            s = jnp.where(inside, s2[:BLK] * scale, -1e30)
            e = jnp.exp(s - jnp.max(s, axis=-1, keepdims=True))
            w = e / jnp.sum(e, axis=-1, keepdims=True)
            sd = (s2[BLK:] + s3) * scale
            wd = w * (sd - jnp.sum(w * sd, axis=-1, keepdims=True))
            wl = w.astype(jnp.bfloat16)
            wb = jnp.concatenate([wl, wd.astype(jnp.bfloat16)], axis=0)
            o2 = lax.dot_general(wb, pad[1, keys, cols], nn, preferred_element_type=jnp.float32)
            o3 = lax.dot_general(wl, pad[3, keys, cols], nn, preferred_element_type=jnp.float32)
            out[0, rows, cols] = o2[:BLK].astype(jnp.bfloat16)
            out[1, rows, cols] = (o2[BLK:] + o3).astype(jnp.bfloat16)
        return carry

    lax.fori_loop(0, tokens // BLK, one_block, 0)


ZD = (0, -1, 1, -2, 2, -3, 3)
YD = (0, -1, 1)


def final_kernel(*refs):
    where, trig = refs[:2]
    ths = refs[2:6]
    ats = refs[6:10]
    lat, noi = refs[10:12]
    zb = refs[12:19]
    z4a, z4b = refs[19:21]
    yb = refs[21:24]
    y2a, y2b = refs[24:26]
    out, tan = refs[26:28]
    wz, wy, sems = refs[28:]
    zi, yi, xi, ti = where[0], where[1], where[2], where[3]

    def place(dst, dz, dy, dx):
        zs = (zi + dz) & 7
        row = (zs & 1) * 640 + ((yi + dy) & 3) * 160 + (xi ^ dx) * 80
        return dst.at[zs >> 1, pl.ds(pl.multiple_of(row, 16), 80)]

    copies = []

    def add(src, dst):
        copies.append(pltpu.make_async_copy(src, dst, sems.at[len(copies)]))

    yd4 = (0, -1, 1, 2)
    zd8 = ZD + (4,)
    for buf, dz in zip(zb, ZD):
        for j, dy in enumerate(yd4):
            for dx in range(2):
                add(buf.at[j, dx], place(wz, dz, dy, dx))
    for half, buf in enumerate((z4a, z4b)):
        for j in range(2):
            for dx in range(2):
                add(buf.at[j, dx], place(wz, 4, yd4[half * 2 + j], dx))
    for buf, dy in zip(yb, YD):
        for j, dz in enumerate(zd8):
            for dx in range(2):
                add(buf.at[j, dx], place(wy, dz, dy, dx))
    for half, buf in enumerate((y2a, y2b)):
        for j in range(4):
            for dx in range(2):
                add(buf.at[j, dx], place(wy, zd8[half * 4 + j], 2, dx))
    for c in copies:
        c.start()
    for c in copies:
        c.wait()
    nt = (((1,), (1,)), ((), ()))
    tokens = lat.shape[0]
    tile = 256
    for n in range(lat.shape[1] // tile):
        cols = slice(n * tile, (n + 1) * tile)
        acc = None
        vel = None
        for j in range(4):
            kb = ti ^ j
            a = ats[j][...].reshape(2 * tokens, ats[j].shape[2])
            p = lax.dot_general(a, wz[kb, cols, :], nt, preferred_element_type=jnp.float32)
            r = lax.dot_general(ths[j][...], wy[kb, cols, :], nt, preferred_element_type=jnp.float32)
            acc = p if acc is None else acc + p
            vel = r if vel is None else vel + r
        for b in range(tokens // BLK):
            rows = slice(b * BLK, (b + 1) * BLK)
            c = trig[0, b]
            s = trig[1, b]
            noisy = c * lat[rows, cols].astype(jnp.float32) + s * noi[rows, cols].astype(jnp.float32)
            br = acc[rows]
            bt = acc[tokens + b * BLK : tokens + (b + 1) * BLK]
            out[rows, cols] = c * noisy - s * br
            tan[rows, cols] = c * vel[rows] - s * noisy - c * br - s * bt


def body(
    latents,
    noise,
    tstep,
    offsets,
    teacher_heads,
    teacher_proj,
    queries,
    keys,
    values,
    query_tangent,
    key_tangent,
    value_tangent,
    out_proj,
):
    tokens, width = queries.shape
    seq = lax.axis_index("seq").astype(jnp.int32)
    tp = lax.axis_index("tp").astype(jnp.int32)
    count = lax.axis_size("seq")
    step_time = (tstep.astype(jnp.float32) + 0.5) * (math.pi / (2 * STEPS))
    trig = jnp.stack([jnp.cos(step_time), jnp.sin(step_time)])
    bf = jnp.bfloat16

    arrays = (keys, values, key_tangent, value_tangent)
    fwd = [(i, i + 1) for i in range(count - 1)]
    bwd = [(i + 1, i) for i in range(count - 1)]
    low = lax.ppermute(jnp.stack([a[tokens - REACH :] for a in arrays]), "seq", fwd)
    high = lax.ppermute(jnp.stack([a[:REACH] for a in arrays]), "seq", bwd)

    small = jnp.stack([out_proj.T, teacher_proj.T])
    p0 = send(small, swap_zt(0))
    p1 = send(small, swap_zt(1))
    oz = jnp.stack([p0[0], p1[0]])
    ty = jnp.stack([p0[1], p1[1]])

    th = [teacher_heads]
    th.append(send(teacher_heads, t_xor(1)))
    th.append(send(teacher_heads, t_xor(2)))
    th.append(send(th[2], t_xor(1)))

    yp = send(oz, y_by(1))
    ym = send(oz, y_by(-1))
    y2 = send(yp, y_by(1))
    zbuf = jnp.stack([oz, yp, ym, y2])
    zp = [ty]
    zm = [ty]
    for _ in range(3):
        zp.append(send(zp[-1], z_by(1)))
        zm.append(send(zm[-1], z_by(-1)))
    z4 = send(zp[3], z_by(1))
    ybuf = jnp.stack([ty, zp[1], zm[1], zp[2], zm[2], zp[3], zm[3], z4])

    y_p = send(ybuf, y_by(1))
    y_m = send(ybuf, y_by(-1))
    y_2a = send(y_p[:4], y_by(1))
    y_2b = send(y_m[4:], y_by(-1))
    zps = [zbuf]
    zms = [zbuf]
    for _ in range(3):
        zps.append(send(zps[-1], z_by(1)))
        zms.append(send(zms[-1], z_by(-1)))
    z_4a = send(zps[3][:2], z_by(1))
    z_4b = send(zms[3][2:], z_by(-1))

    vm = pl.BlockSpec(memory_space=pltpu.VMEM)
    sm = pl.BlockSpec(memory_space=pltpu.SMEM)
    hb = pl.BlockSpec(memory_space=pl.ANY)
    rows = tokens + 2 * REACH
    attended = pl.pallas_call(
        attn_kernel,
        out_shape=jax.ShapeDtypeStruct((2, tokens, width), bf),
        in_specs=[sm, sm, vm, vm] + [hb] * 6,
        out_specs=vm,
        scratch_shapes=[pltpu.VMEM((4, rows, width), bf), pltpu.SemaphoreType.DMA((6,))],
        name="attend",
    )(
        jnp.stack([seq, jnp.int32(count)]),
        offsets,
        queries,
        query_tangent,
        *arrays,
        low,
        high,
    )
    at = [attended]
    at.append(send(attended, t_xor(1)))
    at.append(send(attended, t_xor(2)))
    at.append(send(at[2], t_xor(1)))

    cols = latents.shape[1]
    where = jnp.stack([seq // 8, (seq // 2) % 4, seq % 2, tp])
    f32 = jnp.float32
    return pl.pallas_call(
        final_kernel,
        out_shape=(
            jax.ShapeDtypeStruct((tokens, cols), f32),
            jax.ShapeDtypeStruct((tokens, cols), f32),
        ),
        in_specs=[sm, sm] + [vm] * 10 + [hb] * 14,
        out_specs=(vm, vm),
        scratch_shapes=[
            pltpu.VMEM((NT, cols, width), bf),
            pltpu.VMEM((NT, cols, width), bf),
            pltpu.SemaphoreType.DMA((128,)),
        ],
        name="combine",
    )(
        where,
        trig,
        *th,
        *at,
        latents,
        noise,
        zbuf,
        zps[1],
        zms[1],
        zps[2],
        zms[2],
        zps[3],
        zms[3],
        z_4a,
        z_4b,
        ybuf,
        y_p,
        y_m,
        y_2a,
        y_2b,
    )


def solution(mesh):
    return jax.shard_map(
        body,
        mesh=mesh,
        in_specs=(
            P("seq", "tp"),
            P("seq", "tp"),
            P("seq"),
            P("seq"),
            P("seq", "tp"),
            P("tp", "seq"),
            P("seq", "tp"),
            P("seq", "tp"),
            P("seq", "tp"),
            P("seq", "tp"),
            P("seq", "tp"),
            P("seq", "tp"),
            P("tp", "seq"),
        ),
        out_specs=(P("seq", "tp"), P("seq", "tp")),
        check_vma=False,
    )
```

```python
import functools
import math

import jax
import jax.numpy as jnp
from jax import lax
from jax.experimental import pallas as pl
from jax.experimental.pallas import tpu as pltpu
from jax.sharding import PartitionSpec as P


HD = 128
WIN = 256
OFF = 64
BLK = 64
STEPS = 1000
REACH = WIN // 2 + OFF
AXES = ("seq", "tp")
NZ, NY, NX, NT = 8, 4, 2, 4


def flat(z, y, x, t):
    return (((z % NZ) * NY + y % NY) * NX + x % NX) * NT + t


def pairs(move):
    return [
        (flat(z, y, x, t), flat(*move(z, y, x, t)))
        for z in range(NZ)
        for y in range(NY)
        for x in range(NX)
        for t in range(NT)
    ]


def send(a, move):
    return lax.ppermute(a, AXES, pairs(move))


def z_by(d):
    return lambda z, y, x, t: (z + d, y, x, t)


def y_by(d):
    return lambda z, y, x, t: (z, y + d, x, t)


def t_xor(k):
    return lambda z, y, x, t: (z, y, x, t ^ k)


def swap_zt(flip):
    def move(z, y, x, t):
        m = t ^ (z >> 1)
        return ((z >> 1) * 2 + (m + 1 if z & 1 else -m), y, x ^ flip, z >> 1)

    return move


NT_DIMS = (((1,), (1,)), ((), ()))
NN_DIMS = (((1,), (0,)), ((), ()))
HALF = 640
PAIR = 160
YD = (0, -1, 1, 2)


def attn_kernel(where, offs, q, qd, k, v, kd, vd, low, high, out, pad, sems):
    tokens, width = q.shape
    span = tokens + 2 * REACH
    copies = []
    for n, i in enumerate((0, 2, 1, 3)):
        own = (k, v, kd, vd)[i]
        parts = (
            (own, pad.at[i, pl.ds(REACH, tokens)]),
            (low.at[i], pad.at[i, pl.ds(0, REACH)]),
            (high.at[i], pad.at[i, pl.ds(REACH + tokens, REACH)]),
        )
        for j, (src, dst) in enumerate(parts):
            copies.append(pltpu.make_async_copy(src, dst, sems.at[3 * n + j]))
    for c in copies:
        c.start()
    scale = 1.0 / math.sqrt(HD)
    first = where[0] * tokens
    total = where[1] * tokens
    ki = lax.broadcasted_iota(jnp.int32, (tokens, span), 1) - REACH
    qi = lax.broadcasted_iota(jnp.int32, (tokens, 1), 0)
    off = jnp.zeros((tokens, 1), jnp.int32) + offs[0]
    for b in range(1, tokens // BLK):
        off = jnp.where(qi >= b * BLK, offs[b], off)
    begin = qi + off - WIN // 2
    lower = jnp.maximum(begin, -first)
    upper = jnp.minimum(begin + WIN, total - first)
    inside = (ki >= lower) & (ki < upper)
    for c in copies[:6]:
        c.wait()
    for c in copies[6:]:
        c.wait()

    def head(h, carry):
        cols = pl.ds(pl.multiple_of(h * HD, HD), HD)
        qb = q[:, cols]
        both = jnp.concatenate([qb, qd[:, cols]], axis=0)
        s2 = lax.dot_general(both, pad[0, :, cols], NT_DIMS, preferred_element_type=jnp.float32)
        s3 = lax.dot_general(qb, pad[2, :, cols], NT_DIMS, preferred_element_type=jnp.float32)
        s = jnp.where(inside, s2[:tokens] * scale, -1e30)
        e = jnp.exp(s - jnp.max(s, axis=-1, keepdims=True))
        w = e * (1.0 / jnp.sum(e, axis=-1, keepdims=True))
        sd = (s2[tokens:] + s3) * scale
        wd = w * (sd - jnp.sum(w * sd, axis=-1, keepdims=True))
        wl = w.astype(jnp.bfloat16)
        wb = jnp.concatenate([wl, wd.astype(jnp.bfloat16)], axis=0)
        o2 = lax.dot_general(wb, pad[1, :, cols], NN_DIMS, preferred_element_type=jnp.float32)
        o3 = lax.dot_general(wl, pad[3, :, cols], NN_DIMS, preferred_element_type=jnp.float32)
        out[:tokens, cols] = o2[:tokens].astype(jnp.bfloat16)
        out[tokens:, cols] = (o2[tokens:] + o3).astype(jnp.bfloat16)
        return carry

    lax.fori_loop(0, width // HD, head, 0)


def rows_of(where, dy):
    return pl.ds(pl.multiple_of(((where[1] + dy) & 3) * PAIR, 32), PAIR)


def sources(z, t):
    gap = (z + jnp.array((0, -1, 1, -2, 2, -3, 3, 4), jnp.int32) - 2 * t) & 7
    upper = (gap >= 1) & (gap <= 4)
    return [jnp.where(upper, gap - 1, (8 - gap) & 7), upper.astype(jnp.int32)]


def accumulate(where, x, w, i, acc):
    kb = where[4 + i]
    hf = where[12 + i]
    acc[hf] += lax.dot_general(x[kb], w[i], NT_DIMS, preferred_element_type=jnp.float32)


def tea_kernel(spans, *refs):
    where, vel = refs[0], refs[5 + 4 * len(spans)]
    ths = refs[1:5]
    wy, tea, sem_y, sem_t = refs[-4:]
    heads = [pltpu.make_async_copy(ths[j], tea.at[j], sem_t.at[j]) for j in range(4)]
    for c in heads:
        c.start()
    base = spans[0][0]
    for i, (lo, n) in enumerate(spans):
        for j, dy in enumerate(YD):
            dst = wy.at[pl.ds(lo - base, n), rows_of(where, dy)]
            pltpu.make_async_copy(refs[5 + 4 * i + j], dst, sem_y.at[i]).start()
    if base:
        before, vel = vel, refs[6 + 4 * len(spans)]
        vel[...] = before[...]
    else:
        vel[...] = jnp.zeros_like(vel)
    for c in heads:
        c.wait()
    for i, (lo, n) in enumerate(spans):
        part = wy.at[pl.ds(lo - base, n)]
        pltpu.make_async_copy(part, part, sem_y.at[i]).wait()

        def step(k, carry):
            kb = where[4 + k]
            hf = where[12 + k]
            vel[hf] += lax.dot_general(
                tea[kb], wy[k - base], NT_DIMS, preferred_element_type=jnp.float32
            )
            return carry

        lax.fori_loop(lo, lo + n, step, 0)


def mid_kernel(*refs):
    where = refs[0]
    ats = refs[1:5]
    za = refs[5:12]
    zb = refs[12:19]
    acc = refs[19]
    wz, att, sem_z, sem_a = refs[20:]
    heads = [pltpu.make_async_copy(ats[j], att.at[j], sem_a.at[j]) for j in range(4)]
    for c in heads:
        c.start()
    for i in range(7):
        for j, dy in enumerate(YD):
            buf = (za, zb)[j // 2][i]
            dst = wz.at[i, rows_of(where, dy)]
            pltpu.make_async_copy(buf.at[j % 2], dst, sem_z.at[i]).start()
    acc[...] = jnp.zeros_like(acc)
    for c in heads:
        c.wait()

    def step(k, carry):
        pltpu.make_async_copy(wz.at[k], wz.at[k], sem_z.at[k]).wait()
        accumulate(where, att, wz, k, acc)
        return carry

    lax.fori_loop(0, 7, step, 0)


def last_kernel(*refs):
    where, trig = refs[:2]
    ats = refs[2:6]
    z4 = refs[6:8]
    more = refs[8:10]
    acc, vel = refs[10:12]
    outs = refs[12:14]
    wz, att, lat, noi, p, res, sem_z, sem_a, sem_m, sem_o = refs[14:]
    kb = where[11]
    for j, dy in enumerate(YD):
        pltpu.make_async_copy(z4[j // 2].at[j % 2], wz.at[rows_of(where, dy)], sem_z.at[0]).start()
    for j in range(4):

        @pl.when(kb == j)
        def _():
            pltpu.make_async_copy(ats[j], att, sem_a.at[0]).start()

    extra = [
        pltpu.make_async_copy(s, d, sem_m.at[i]) for i, (s, d) in enumerate(zip(more, (lat, noi)))
    ]
    for c in extra:
        c.start()
    pltpu.make_async_copy(ats[0], att, sem_a.at[0]).wait()
    pltpu.make_async_copy(wz, wz, sem_z.at[0]).wait()
    p[...] = lax.dot_general(att[...], wz[...], NT_DIMS, preferred_element_type=jnp.float32)
    for c in extra:
        c.wait()
    tokens = lat.shape[0]
    stores = []
    for hf in range(2):
        cols = slice(hf * HALF, (hf + 1) * HALF)
        on = (where[19] == hf).astype(jnp.float32)

        def block(b, carry):
            start = pl.multiple_of(b * BLK, BLK)
            rows = pl.ds(start, BLK)
            low = pl.ds(pl.multiple_of(tokens + start, BLK), BLK)
            c = trig[0, b]
            s = trig[1, b]
            noisy = c * lat[rows, cols].astype(jnp.float32) + s * noi[rows, cols].astype(jnp.float32)
            br = acc[hf, rows] + on * p[rows]
            bt = acc[hf, low] + on * p[low]
            res[0, hf, rows] = c * noisy - s * br
            res[1, hf, rows] = c * vel[hf, rows] - s * noisy - c * br - s * bt
            return carry

        lax.fori_loop(0, tokens // BLK, block, 0)
        for k in range(2):
            dst = outs[k].at[:, pl.ds(hf * HALF, HALF)]
            stores.append(pltpu.make_async_copy(res.at[k, hf], dst, sem_o.at[2 * hf + k]))
            stores[-1].start()
    for c in stores:
        c.wait()


def body(
    latents,
    noise,
    tstep,
    offsets,
    teacher_heads,
    teacher_proj,
    queries,
    keys,
    values,
    query_tangent,
    key_tangent,
    value_tangent,
    out_proj,
):
    tokens, width = queries.shape
    seq = lax.axis_index("seq").astype(jnp.int32)
    tp = lax.axis_index("tp").astype(jnp.int32)
    count = lax.axis_size("seq")
    step_time = (tstep.astype(jnp.float32) + 0.5) * (math.pi / (2 * STEPS))
    trig = jnp.stack([jnp.cos(step_time), jnp.sin(step_time)])
    bf = jnp.bfloat16

    arrays = (keys, values, key_tangent, value_tangent)
    fwd = [(i, i + 1) for i in range(count - 1)]
    bwd = [(i + 1, i) for i in range(count - 1)]
    low = lax.ppermute(jnp.stack([a[tokens - REACH :] for a in arrays]), "seq", fwd)
    high = lax.ppermute(jnp.stack([a[:REACH] for a in arrays]), "seq", bwd)

    small = jnp.stack([out_proj.T, teacher_proj.T])
    p0 = send(small, swap_zt(0))
    p1 = send(small, swap_zt(1))
    even = seq % 2 == 0
    unit = jnp.concatenate([jnp.where(even, p0, p1), jnp.where(even, p1, p0)], axis=1)
    oz = unit[0]
    ty = unit[1]

    th = [teacher_heads]
    th.append(send(teacher_heads, t_xor(1)))
    th.append(send(teacher_heads, t_xor(2)))
    th.append(send(th[2], t_xor(1)))

    yp = send(oz, y_by(1))
    ym = send(oz, y_by(-1))
    y2 = send(yp, y_by(1))

    def over_z(buf, up):
        p = [buf]
        m = [buf]
        for _ in range(3):
            p.append(send(p[-1], z_by(1)))
            m.append(send(m[-1], z_by(-1)))
        end = send(p[3] if up else m[3], z_by(1 if up else -1))
        return [buf, p[1], m[1], p[2], m[2], p[3], m[3]], end

    za, za4 = over_z(jnp.stack([oz, yp]), True)
    zb, zb4 = over_z(jnp.stack([ym, y2]), False)

    zp = [ty]
    zm = [ty]
    for _ in range(3):
        zp.append(send(zp[-1], z_by(1)))
        zm.append(send(zm[-1], z_by(-1)))
    z4 = send(zp[3], z_by(1))

    def over_y(parts, up):
        buf = jnp.stack(parts)
        p = send(buf, y_by(1))
        m = send(buf, y_by(-1))
        end = send(p if up else m, y_by(1 if up else -1))
        return [buf, p, m, end]

    sets = over_y([ty, zp[1], zm[1]], False)
    sets += over_y([zp[2], zm[2]], True)
    sets += over_y([zp[3], zm[3], z4], True)

    vm = pl.BlockSpec(memory_space=pltpu.VMEM)
    sm = pl.BlockSpec(memory_space=pltpu.SMEM)
    hb = pl.BlockSpec(memory_space=pl.ANY)
    dma = pltpu.SemaphoreType.DMA
    f32 = jnp.float32
    attended = pl.pallas_call(
        attn_kernel,
        out_shape=jax.ShapeDtypeStruct((2 * tokens, width), bf),
        in_specs=[sm, sm, vm, vm] + [hb] * 6,
        out_specs=vm,
        scratch_shapes=[pltpu.VMEM((4, tokens + 2 * REACH, width), bf), dma((12,))],
        compiler_params=pltpu.CompilerParams(vmem_limit_bytes=20 << 20),
        name="attend",
    )(
        jnp.stack([seq, jnp.int32(count)]),
        offsets,
        queries,
        query_tangent,
        *arrays,
        low,
        high,
    )
    at = [attended]
    at.append(send(attended, t_xor(1)))
    at.append(send(attended, t_xor(2)))
    at.append(send(at[2], t_xor(1)))

    cols = latents.shape[1]
    where = jnp.concatenate(
        [jnp.stack([seq // 8, (seq // 2) % 4, seq % 2, tp])] + sources(seq // 8, tp)
    )
    full = jax.ShapeDtypeStruct((2, 2 * tokens, HALF), f32)
    half = jax.ShapeDtypeStruct((2, tokens, HALF), f32)

    def run(kernel, out_shape, ins, specs, outs, scratch):
        return pl.pallas_call(
            kernel,
            out_shape=out_shape,
            in_specs=specs,
            out_specs=outs,
            scratch_shapes=scratch,
            compiler_params=pltpu.CompilerParams(vmem_limit_bytes=16 << 20),
        )(*ins)

    def teach(spans, bufs, *before):
        total = sum(n for _, n in spans)
        return run(
            functools.partial(tea_kernel, spans),
            half,
            (where, *th, *bufs, *before),
            [sm] + [hb] * (4 + len(bufs)) + [vm] * len(before),
            vm,
            [
                pltpu.VMEM((total, HALF, width), bf),
                pltpu.VMEM((4, tokens, width), bf),
                dma((len(spans),)),
                dma((4,)),
            ],
        )

    vel = teach(SPANS[:CUT], sets[: 4 * CUT])
    vel = teach(SPANS[CUT:], sets[4 * CUT :], vel)
    acc = run(
        mid_kernel,
        full,
        (where, *at, *za, *zb),
        [sm] + [hb] * 18,
        vm,
        [
            pltpu.VMEM((7, HALF, width), bf),
            pltpu.VMEM((4, 2 * tokens, width), bf),
            dma((7,)),
            dma((4,)),
        ],
    )
    return run(
        last_kernel,
        (jax.ShapeDtypeStruct((tokens, cols), f32),) * 2,
        (where, trig, *at, za4, zb4, latents, noise, acc, vel),
        [sm, sm] + [hb] * 8 + [vm] * 2,
        (hb, hb),
        [
            pltpu.VMEM((HALF, width), bf),
            pltpu.VMEM((2 * tokens, width), bf),
            pltpu.VMEM((tokens, cols), bf),
            pltpu.VMEM((tokens, cols), bf),
            pltpu.VMEM((2 * tokens, HALF), f32),
            pltpu.VMEM((2, 2, tokens, HALF), f32),
            dma((1,)),
            dma((1,)),
            dma((2,)),
            dma((4,)),
        ],
    )


SPANS = ((0, 3), (3, 2), (5, 3))
CUT = 2


def solution(mesh):
    return jax.shard_map(
        body,
        mesh=mesh,
        in_specs=(
            P("seq", "tp"),
            P("seq", "tp"),
            P("seq"),
            P("seq"),
            P("seq", "tp"),
            P("tp", "seq"),
            P("seq", "tp"),
            P("seq", "tp"),
            P("seq", "tp"),
            P("seq", "tp"),
            P("seq", "tp"),
            P("seq", "tp"),
            P("tp", "seq"),
        ),
        out_specs=(P("seq", "tp"), P("seq", "tp")),
        check_vma=False,
    )
```

```python
import functools
import math

import jax
import jax.numpy as jnp
from jax import lax
from jax.experimental import pallas as pl
from jax.experimental.pallas import tpu as pltpu
from jax.sharding import PartitionSpec as P


HD = 128
WIN = 256
OFF = 64
BLK = 64
STEPS = 1000
REACH = WIN // 2 + OFF
AXES = ("seq", "tp")
NZ, NY, NX, NT = 8, 4, 2, 4


def flat(z, y, x, t):
    return (((z % NZ) * NY + y % NY) * NX + x % NX) * NT + t


def pairs(move):
    return [
        (flat(z, y, x, t), flat(*move(z, y, x, t)))
        for z in range(NZ)
        for y in range(NY)
        for x in range(NX)
        for t in range(NT)
    ]


def send(a, move):
    return lax.ppermute(a, AXES, pairs(move))


def z_by(d):
    return lambda z, y, x, t: (z + d, y, x, t)


def y_by(d):
    return lambda z, y, x, t: (z, y + d, x, t)


def t_xor(k):
    return lambda z, y, x, t: (z, y, x, t ^ k)


def swap_zt(flip):
    def move(z, y, x, t):
        m = t ^ (z >> 1)
        return ((z >> 1) * 2 + (m + 1 if z & 1 else -m), y, x ^ flip, z >> 1)

    return move


NT_DIMS = (((1,), (1,)), ((), ()))
NN_DIMS = (((1,), (0,)), ((), ()))
HALF = 640
PAIR = 160
YD = (0, -1, 1, 2)


def attn_kernel(where, offs, q, qd, k, v, kd, vd, low, high, out, pad, sems):
    tokens, width = q.shape
    span = tokens + 2 * REACH
    copies = []
    for n, i in enumerate((0, 2, 1, 3)):
        own = (k, v, kd, vd)[i]
        parts = (
            (own, pad.at[i, pl.ds(REACH, tokens)]),
            (low.at[i], pad.at[i, pl.ds(0, REACH)]),
            (high.at[i], pad.at[i, pl.ds(REACH + tokens, REACH)]),
        )
        for j, (src, dst) in enumerate(parts):
            copies.append(pltpu.make_async_copy(src, dst, sems.at[3 * n + j]))
    for c in copies:
        c.start()
    scale = 1.0 / math.sqrt(HD)
    first = where[0] * tokens
    total = where[1] * tokens
    ki = lax.broadcasted_iota(jnp.int32, (tokens, span), 1) - REACH
    qi = lax.broadcasted_iota(jnp.int32, (tokens, 1), 0)
    off = jnp.zeros((tokens, 1), jnp.int32) + offs[0]
    for b in range(1, tokens // BLK):
        off = jnp.where(qi >= b * BLK, offs[b], off)
    begin = qi + off - WIN // 2
    lower = jnp.maximum(begin, -first)
    upper = jnp.minimum(begin + WIN, total - first)
    inside = (ki >= lower) & (ki < upper)
    for c in copies[:6]:
        c.wait()
    for c in copies[6:]:
        c.wait()

    def head(h, carry):
        cols = pl.ds(pl.multiple_of(h * HD, HD), HD)
        qb = q[:, cols]
        both = jnp.concatenate([qb, qd[:, cols]], axis=0)
        s2 = lax.dot_general(both, pad[0, :, cols], NT_DIMS, preferred_element_type=jnp.float32)
        s3 = lax.dot_general(qb, pad[2, :, cols], NT_DIMS, preferred_element_type=jnp.float32)
        s = jnp.where(inside, s2[:tokens] * scale, -1e30)
        e = jnp.exp(s - jnp.max(s, axis=-1, keepdims=True))
        w = e * (1.0 / jnp.sum(e, axis=-1, keepdims=True))
        sd = (s2[tokens:] + s3) * scale
        wd = w * (sd - jnp.sum(w * sd, axis=-1, keepdims=True))
        wl = w.astype(jnp.bfloat16)
        wb = jnp.concatenate([wl, wd.astype(jnp.bfloat16)], axis=0)
        o2 = lax.dot_general(wb, pad[1, :, cols], NN_DIMS, preferred_element_type=jnp.float32)
        o3 = lax.dot_general(wl, pad[3, :, cols], NN_DIMS, preferred_element_type=jnp.float32)
        out[:tokens, cols] = o2[:tokens].astype(jnp.bfloat16)
        out[tokens:, cols] = (o2[tokens:] + o3).astype(jnp.bfloat16)
        return carry

    lax.fori_loop(0, width // HD, head, 0)


def rows_of(where, dy):
    return pl.ds(pl.multiple_of(((where[1] + dy) & 3) * PAIR, 32), PAIR)


def sources(z, t):
    gap = (z + jnp.array((0, -1, 1, -2, 2, -3, 3, 4), jnp.int32) - 2 * t) & 7
    upper = (gap >= 1) & (gap <= 4)
    return [jnp.where(upper, gap - 1, (8 - gap) & 7), upper.astype(jnp.int32)]


def accumulate(where, x, w, i, acc):
    kb = where[4 + i]
    hf = where[12 + i]
    acc[hf] += lax.dot_general(x[kb], w[i], NT_DIMS, preferred_element_type=jnp.float32)


def tea_kernel(spans, *refs):
    where, vel = refs[0], refs[5 + 4 * len(spans)]
    ths = refs[1:5]
    wy, tea, sem_y, sem_t = refs[-4:]
    heads = [pltpu.make_async_copy(ths[j], tea.at[j], sem_t.at[j]) for j in range(4)]
    for c in heads:
        c.start()
    base = spans[0][0]
    for i, (lo, n) in enumerate(spans):
        for j, dy in enumerate(YD):
            dst = wy.at[pl.ds(lo - base, n), rows_of(where, dy)]
            pltpu.make_async_copy(refs[5 + 4 * i + j], dst, sem_y.at[i]).start()
    if base:
        before, vel = vel, refs[6 + 4 * len(spans)]
        vel[...] = before[...]
    else:
        vel[...] = jnp.zeros_like(vel)
    for c in heads:
        c.wait()
    for i, (lo, n) in enumerate(spans):
        part = wy.at[pl.ds(lo - base, n)]
        pltpu.make_async_copy(part, part, sem_y.at[i]).wait()

        def step(k, carry):
            kb = where[4 + k]
            hf = where[12 + k]
            vel[hf] += lax.dot_general(
                tea[kb], wy[k - base], NT_DIMS, preferred_element_type=jnp.float32
            )
            return carry

        lax.fori_loop(lo, lo + n, step, 0)


def mid_kernel(*refs):
    where = refs[0]
    ths = refs[1:5]
    ats = refs[5:9]
    rest = refs[9:13]
    za = refs[13:20]
    zb = refs[20:27]
    before, acc, vel = refs[27:30]
    wz, wy, att, tea, sem_z, sem_y, sem_a, sem_t = refs[30:]
    lo, n = SPANS[2]
    heads = [pltpu.make_async_copy(ths[j], tea.at[j], sem_t.at[j]) for j in range(4)]
    for c in heads:
        c.start()
    for j, dy in enumerate(YD):
        dst = wy.at[pl.ds(0, n), rows_of(where, dy)]
        pltpu.make_async_copy(rest[j], dst, sem_y.at[0]).start()
    more = [pltpu.make_async_copy(ats[j], att.at[j], sem_a.at[j]) for j in range(4)]
    for c in more:
        c.start()
    for i in range(7):
        for j, dy in enumerate(YD):
            buf = (za, zb)[j // 2][i]
            dst = wz.at[i, rows_of(where, dy)]
            pltpu.make_async_copy(buf.at[j % 2], dst, sem_z.at[i]).start()
    vel[...] = before[...]
    acc[...] = jnp.zeros_like(acc)
    for c in heads:
        c.wait()
    pltpu.make_async_copy(wy, wy, sem_y.at[0]).wait()

    def teach(k, carry):
        kb = where[4 + lo + k]
        hf = where[12 + lo + k]
        vel[hf] += lax.dot_general(tea[kb], wy[k], NT_DIMS, preferred_element_type=jnp.float32)
        return carry

    lax.fori_loop(0, n, teach, 0)
    for c in more:
        c.wait()

    def step(k, carry):
        pltpu.make_async_copy(wz.at[k], wz.at[k], sem_z.at[k]).wait()
        accumulate(where, att, wz, k, acc)
        return carry

    lax.fori_loop(0, 7, step, 0)


def last_kernel(*refs):
    where, trig = refs[:2]
    ats = refs[2:6]
    z4 = refs[6:8]
    more = refs[8:10]
    acc, vel = refs[10:12]
    outs = refs[12:14]
    wz, att, lat, noi, p, res, sem_z, sem_a, sem_m, sem_o = refs[14:]
    kb = where[11]
    for j, dy in enumerate(YD):
        pltpu.make_async_copy(z4[j // 2].at[j % 2], wz.at[rows_of(where, dy)], sem_z.at[0]).start()
    for j in range(4):

        @pl.when(kb == j)
        def _():
            pltpu.make_async_copy(ats[j], att, sem_a.at[0]).start()

    extra = [
        pltpu.make_async_copy(s, d, sem_m.at[i]) for i, (s, d) in enumerate(zip(more, (lat, noi)))
    ]
    for c in extra:
        c.start()
    pltpu.make_async_copy(ats[0], att, sem_a.at[0]).wait()
    pltpu.make_async_copy(wz, wz, sem_z.at[0]).wait()
    p[...] = lax.dot_general(att[...], wz[...], NT_DIMS, preferred_element_type=jnp.float32)
    for c in extra:
        c.wait()
    tokens = lat.shape[0]
    stores = []
    for hf in range(2):
        cols = slice(hf * HALF, (hf + 1) * HALF)
        on = (where[19] == hf).astype(jnp.float32)

        def block(b, carry):
            start = pl.multiple_of(b * BLK, BLK)
            rows = pl.ds(start, BLK)
            low = pl.ds(pl.multiple_of(tokens + start, BLK), BLK)
            c = trig[0, b]
            s = trig[1, b]
            noisy = c * lat[rows, cols].astype(jnp.float32) + s * noi[rows, cols].astype(jnp.float32)
            br = acc[hf, rows] + on * p[rows]
            bt = acc[hf, low] + on * p[low]
            res[0, hf, rows] = c * noisy - s * br
            res[1, hf, rows] = c * vel[hf, rows] - s * noisy - c * br - s * bt
            return carry

        lax.fori_loop(0, tokens // BLK, block, 0)
        for k in range(2):
            dst = outs[k].at[:, pl.ds(hf * HALF, HALF)]
            stores.append(pltpu.make_async_copy(res.at[k, hf], dst, sem_o.at[2 * hf + k]))
            stores[-1].start()
    for c in stores:
        c.wait()


def body(
    latents,
    noise,
    tstep,
    offsets,
    teacher_heads,
    teacher_proj,
    queries,
    keys,
    values,
    query_tangent,
    key_tangent,
    value_tangent,
    out_proj,
):
    tokens, width = queries.shape
    seq = lax.axis_index("seq").astype(jnp.int32)
    tp = lax.axis_index("tp").astype(jnp.int32)
    count = lax.axis_size("seq")
    step_time = (tstep.astype(jnp.float32) + 0.5) * (math.pi / (2 * STEPS))
    trig = jnp.stack([jnp.cos(step_time), jnp.sin(step_time)])
    bf = jnp.bfloat16

    arrays = (keys, values, key_tangent, value_tangent)
    fwd = [(i, i + 1) for i in range(count - 1)]
    bwd = [(i + 1, i) for i in range(count - 1)]
    low = lax.ppermute(jnp.stack([a[tokens - REACH :] for a in arrays]), "seq", fwd)
    high = lax.ppermute(jnp.stack([a[:REACH] for a in arrays]), "seq", bwd)

    small = jnp.stack([out_proj.T, teacher_proj.T])
    p0 = send(small, swap_zt(0))
    p1 = send(small, swap_zt(1))
    even = seq % 2 == 0
    unit = jnp.concatenate([jnp.where(even, p0, p1), jnp.where(even, p1, p0)], axis=1)
    oz = unit[0]
    ty = unit[1]

    th = [teacher_heads]
    th.append(send(teacher_heads, t_xor(1)))
    th.append(send(teacher_heads, t_xor(2)))
    th.append(send(th[2], t_xor(1)))

    yp = send(oz, y_by(1))
    ym = send(oz, y_by(-1))
    y2 = send(yp, y_by(1))

    def over_z(buf, up):
        p = [buf]
        m = [buf]
        for _ in range(3):
            p.append(send(p[-1], z_by(1)))
            m.append(send(m[-1], z_by(-1)))
        end = send(p[3] if up else m[3], z_by(1 if up else -1))
        return [buf, p[1], m[1], p[2], m[2], p[3], m[3]], end

    za, za4 = over_z(jnp.stack([oz, yp]), True)
    zb, zb4 = over_z(jnp.stack([ym, y2]), False)

    zp = [ty]
    zm = [ty]
    for _ in range(3):
        zp.append(send(zp[-1], z_by(1)))
        zm.append(send(zm[-1], z_by(-1)))
    z4 = send(zp[3], z_by(1))

    def over_y(parts, up):
        buf = jnp.stack(parts)
        p = send(buf, y_by(1))
        m = send(buf, y_by(-1))
        end = send(p if up else m, y_by(1 if up else -1))
        return [buf, p, m, end]

    sets = over_y([ty, zp[1], zm[1]], False)
    sets += over_y([zp[2], zm[2]], True)
    sets += over_y([zp[3], zm[3], z4], True)

    vm = pl.BlockSpec(memory_space=pltpu.VMEM)
    sm = pl.BlockSpec(memory_space=pltpu.SMEM)
    hb = pl.BlockSpec(memory_space=pl.ANY)
    dma = pltpu.SemaphoreType.DMA
    f32 = jnp.float32
    attended = pl.pallas_call(
        attn_kernel,
        out_shape=jax.ShapeDtypeStruct((2 * tokens, width), bf),
        in_specs=[sm, sm, vm, vm] + [hb] * 6,
        out_specs=vm,
        scratch_shapes=[pltpu.VMEM((4, tokens + 2 * REACH, width), bf), dma((12,))],
        compiler_params=pltpu.CompilerParams(vmem_limit_bytes=20 << 20),
        name="attend",
    )(
        jnp.stack([seq, jnp.int32(count)]),
        offsets,
        queries,
        query_tangent,
        *arrays,
        low,
        high,
    )
    at = [attended]
    at.append(send(attended, t_xor(1)))
    at.append(send(attended, t_xor(2)))
    at.append(send(at[2], t_xor(1)))

    cols = latents.shape[1]
    where = jnp.concatenate(
        [jnp.stack([seq // 8, (seq // 2) % 4, seq % 2, tp])] + sources(seq // 8, tp)
    )
    full = jax.ShapeDtypeStruct((2, 2 * tokens, HALF), f32)
    half = jax.ShapeDtypeStruct((2, tokens, HALF), f32)

    def run(kernel, out_shape, ins, specs, outs, scratch, grant=16):
        return pl.pallas_call(
            kernel,
            out_shape=out_shape,
            in_specs=specs,
            out_specs=outs,
            scratch_shapes=scratch,
            compiler_params=pltpu.CompilerParams(vmem_limit_bytes=grant << 20),
        )(*ins)

    def teach(spans, bufs, *before):
        total = sum(n for _, n in spans)
        return run(
            functools.partial(tea_kernel, spans),
            half,
            (where, *th, *bufs, *before),
            [sm] + [hb] * (4 + len(bufs)) + [vm] * len(before),
            vm,
            [
                pltpu.VMEM((total, HALF, width), bf),
                pltpu.VMEM((4, tokens, width), bf),
                dma((len(spans),)),
                dma((4,)),
            ],
        )

    vel = teach(SPANS[:CUT], sets[: 4 * CUT])
    acc, vel = run(
        mid_kernel,
        (full, half),
        (where, *th, *at, *sets[8:], *za, *zb, vel),
        [sm] + [hb] * 26 + [vm],
        (vm, vm),
        [
            pltpu.VMEM((7, HALF, width), bf),
            pltpu.VMEM((3, HALF, width), bf),
            pltpu.VMEM((4, 2 * tokens, width), bf),
            pltpu.VMEM((4, tokens, width), bf),
            dma((7,)),
            dma((1,)),
            dma((4,)),
            dma((4,)),
        ],
        19,
    )
    return run(
        last_kernel,
        (jax.ShapeDtypeStruct((tokens, cols), f32),) * 2,
        (where, trig, *at, za4, zb4, latents, noise, acc, vel),
        [sm, sm] + [hb] * 8 + [vm] * 2,
        (hb, hb),
        [
            pltpu.VMEM((HALF, width), bf),
            pltpu.VMEM((2 * tokens, width), bf),
            pltpu.VMEM((tokens, cols), bf),
            pltpu.VMEM((tokens, cols), bf),
            pltpu.VMEM((2 * tokens, HALF), f32),
            pltpu.VMEM((2, 2, tokens, HALF), f32),
            dma((1,)),
            dma((1,)),
            dma((2,)),
            dma((4,)),
        ],
    )


SPANS = ((0, 3), (3, 2), (5, 3))
CUT = 2


def solution(mesh):
    return jax.shard_map(
        body,
        mesh=mesh,
        in_specs=(
            P("seq", "tp"),
            P("seq", "tp"),
            P("seq"),
            P("seq"),
            P("seq", "tp"),
            P("tp", "seq"),
            P("seq", "tp"),
            P("seq", "tp"),
            P("seq", "tp"),
            P("seq", "tp"),
            P("seq", "tp"),
            P("seq", "tp"),
            P("tp", "seq"),
        ),
        out_specs=(P("seq", "tp"), P("seq", "tp")),
        check_vma=False,
    )
```
